256 devices in a mesh: grp: 4 (over y), tok: 64 (over z, x, core).
Axes of the slice: x: 4, y: 4, z: 8, core: 2. Of those that a mesh axis runs over, the one named last changes fastest.
Arguments:
- queries: bfloat16 [32768, 768], P(('grp', 'tok')), may hold values from -6 to 6
- key_tokens: float32 [32768, 768], P(('grp', 'tok')), may hold values from -6 to 6
- values: float32 [32768, 768], P(('grp', 'tok')), may hold values from -6 to 6
- out_grad: bfloat16 [32768, 768], P(('grp', 'tok')), may hold values from -6 to 6
- w_gate: float32 [768, 768], replicated, may hold values from -0.21875 to 0.21875
- w_up: float32 [768, 768], replicated, may hold values from -0.21875 to 0.21875
- w_down: float32 [768, 768], replicated, may hold values from -0.21875 to 0.21875
Outputs:
- d_queries: bfloat16 [32768, 768], P(('grp', 'tok'))
- d_keys: float32 [32768, 768], P(('grp', 'tok'))
- d_values: float32 [32768, 768], P(('grp', 'tok'))
- d_gate: float32 [768, 768], P('tok')
- d_up: float32 [768, 768], P('tok')
- d_down: float32 [768, 768], P('tok')
The draws below stay inside these ranges and needn't reach their ends.
All inputs are finite; a program needn't handle non-finite values.
Results may differ from the reference program's by a relative error of at most 0.012.
Values may be sent and summed in bfloat16 or wider, within the bound.
No kernel may reach another device: no remote copies, remote signals or barrier semaphores. Data moves between devices by JAX's collectives and lax.ppermute only.
A program may use at most 128 MiB of HBM per device.

```python
import jax
import jax.numpy as jnp
from jax import lax

D = 768
TOK_DEV = 128
TOKENS = 32768


def block_scale(key, dims, pieces, low, high):
    def one(axis_at, shards_of):
        steps = jax.random.uniform(jax.random.fold_in(jax.random.fold_in(key, 6), axis_at), (shards_of,), jnp.float32, low / len(pieces), high / len(pieces))
        return jnp.repeat(jnp.exp(steps), dims[axis_at] // shards_of).reshape((-1,) + (1,) * (len(dims) - axis_at - 1))

    gain = one(*pieces[0])
    for cut in pieces[1:]:
        gain = gain * one(*cut)
    return gain


def centred(key, dims, width, limit, shards=(), kind=jnp.bfloat16):
    values = jax.random.normal(key, dims, jnp.float32) * width
    if len(shards) > 0:
        values = block_scale(key, dims, shards, -0.22, 0.18) * values
    return jnp.clip(values, min=-limit, max=limit).astype(kind)


def setup_inputs(seed: int = 0) -> dict:
    keys = jax.random.split(jax.random.key(seed), 8)
    return {
        "queries": centred(keys[0], (TOKENS, D), 1.0, 6.0, ((0, 256),)),
        "key_tokens": centred(keys[1], (TOKENS, D), 1.0, 6.0, ((0, 256),), jnp.float32),
        "values": centred(keys[2], (TOKENS, D), 1.0, 6.0, ((0, 256),), jnp.float32),
        "out_grad": centred(keys[3], (TOKENS, D), 1.0, 6.0, ((0, 256),)),
        "w_gate": centred(keys[4], (D, D), D ** -0.5, 0.21875, (), jnp.float32),
        "w_up": centred(keys[5], (D, D), D ** -0.5, 0.21875, (), jnp.float32),
        "w_down": centred(keys[6], (D, D), D ** -0.5, 0.21875, (), jnp.float32),
    }


STEP_SIZE = 0.02
EPSILON = 1e-06
HIGH = lax.Precision.HIGHEST

def matmul(left, right):
    return jnp.dot(left, right, precision=HIGH, preferred_element_type=jnp.float32)

def key_grad(w_gate, w_up, w_down, key_rows, value_rows):
    hidden_gate = matmul(key_rows, w_gate)
    hidden_up = matmul(key_rows, w_up)
    sig = jax.nn.sigmoid(hidden_gate)
    active = hidden_gate * sig * hidden_up
    error = matmul(active, w_down) - value_rows
    d_active = matmul(error, w_down.T)
    d_hup = d_active * hidden_gate * sig
    d_hgate = d_active * hidden_up * sig * (1.0 + hidden_gate * (1.0 - sig))
    return (matmul(key_rows.T, d_hgate), matmul(key_rows.T, d_hup), matmul(active.T, error))

def query_grad(fast_weights, query_rows, grad_rows):
    fast_gate, fast_up, fast_down = fast_weights
    hidden_gate = jnp.dot(query_rows, fast_gate, preferred_element_type=jnp.float32)
    hidden_up = jnp.dot(query_rows, fast_up, preferred_element_type=jnp.float32)
    sig = jax.nn.sigmoid(hidden_gate)
    active = (hidden_gate * sig * hidden_up).astype(jnp.bfloat16)
    d_active = jnp.dot(grad_rows, fast_down.T, preferred_element_type=jnp.float32)
    d_hup = (d_active * hidden_gate * sig).astype(jnp.bfloat16)
    d_hgate = (d_active * hidden_up * sig * (1.0 + hidden_gate * (1.0 - sig))).astype(jnp.bfloat16)
    d_rows = (jnp.dot(d_hgate, fast_gate.T, preferred_element_type=jnp.float32) + jnp.dot(d_hup, fast_up.T, preferred_element_type=jnp.float32)).astype(jnp.bfloat16)
    grads = (jnp.dot(query_rows.T, d_hgate, preferred_element_type=jnp.float32), jnp.dot(query_rows.T, d_hup, preferred_element_type=jnp.float32), jnp.dot(active.T, grad_rows, preferred_element_type=jnp.float32))
    return (d_rows, grads)

def column_sums(matrices):
    return tuple((lax.optimization_barrier(jnp.sum(matrix * matrix, axis=0)) for matrix in matrices))

def apply_update(weight_rows, grad_parts, squares, full_width):
    scales = tuple((jnp.sqrt(square / full_width + EPSILON) for square in squares))
    fast_weights = tuple(((weight - STEP_SIZE * grad / scale).astype(jnp.bfloat16) for weight, grad, scale in zip(weight_rows, grad_parts, scales)))
    return (fast_weights, scales)

def back_products(query_parts, grad_parts):
    return tuple((lax.optimization_barrier(jnp.sum(-STEP_SIZE * dpart * gpart, axis=0)) for dpart, gpart in zip(query_parts, grad_parts)))

def normal_back(query_parts, grad_parts, scales, products, full_width):
    return tuple(((-STEP_SIZE * dpart / scale - gpart * product / (full_width * scale * scale * scale)).astype(jnp.bfloat16) for dpart, gpart, scale, product in zip(query_parts, grad_parts, scales, products)))

def reference(queries, key_tokens, values, out_grad, w_gate, w_up, w_down):
    weights = (w_gate, w_up, w_down)
    full_width = w_gate.shape[0]
    key_blocks = key_tokens.reshape(-1, TOK_DEV, full_width)
    value_blocks = values.reshape(-1, TOK_DEV, full_width)
    query_blocks = queries.reshape(-1, TOK_DEV, full_width)
    grad_blocks = out_grad.reshape(-1, TOK_DEV, full_width)
    zeros = tuple((jnp.zeros((full_width, full_width), jnp.float32) for weight in weights))

    def forward_step(summed, block):
        local = key_grad(w_gate, w_up, w_down, block[0], block[1])
        return (tuple((left + right for left, right in zip(summed, local))), None)
    grad_sum, unused = lax.scan(forward_step, zeros, (key_blocks, value_blocks))
    fast_weights, scales = apply_update(weights, grad_sum, column_sums(grad_sum), full_width)

    def query_step(summed, block):
        d_rows, local = query_grad(fast_weights, block[0], block[1])
        return (tuple((left + right for left, right in zip(summed, local))), d_rows)
    query_sum, d_query_blocks = lax.scan(query_step, zeros, (query_blocks, grad_blocks))
    rounded = normal_back(query_sum, grad_sum, scales, back_products(query_sum, grad_sum), full_width)
    rounded = lax.optimization_barrier(rounded)
    cotangent = tuple((item.astype(jnp.float32) for item in rounded))

    def second_step(summed, block):
        unused_out, pullback = jax.vjp(key_grad, w_gate, w_up, w_down, block[0], block[1])
        grads = pullback(cotangent)
        return (tuple((left + right for left, right in zip(summed, grads[:3]))), (grads[3], grads[4]))
    second_sum, pair = lax.scan(second_step, zeros, (key_blocks, value_blocks))
    inverse = 1.0 / TOKENS
    summed = tuple(((left + right) * inverse for left, right in zip(query_sum, second_sum)))
    return (d_query_blocks.reshape(-1, full_width), pair[0].reshape(-1, full_width), pair[1].reshape(-1, full_width), summed[0], summed[1], summed[2])
```

```python
import jax
import jax.numpy as jnp
import numpy as np
from jax import lax
from jax.experimental import pallas as pl
from jax.experimental.pallas import tpu as pltpu
from jax.sharding import Mesh, PartitionSpec as P

STEP_SIZE = 0.02
EPSILON = 1e-06
HIGH = lax.Precision.HIGHEST
F32 = jnp.float32
BF16 = jnp.bfloat16

NY, NZ, NX, NC = 4, 8, 4, 2
D = 768
BLK = D // (NC * NX * NY)
OWN = BLK // NZ
PAD = 16
XY = NX * NY

VM = pl.BlockSpec(memory_space=pltpu.VMEM)
SM = pl.BlockSpec(memory_space=pltpu.SMEM)


def call(kernel, outs, *args, scalars=0, flops=0):
    outs = tuple(jax.ShapeDtypeStruct(s, d) for s, d in outs)
    size = sum(int(np.prod(a.shape)) * a.dtype.itemsize for a in (*args, *outs))
    return pl.pallas_call(
        kernel,
        out_shape=outs,
        in_specs=[SM] * scalars + [VM] * (len(args) - scalars),
        out_specs=tuple(VM for _ in outs),
        compiler_params=pltpu.CompilerParams(vmem_limit_bytes=48 * 1024 * 1024),
        cost_estimate=pl.CostEstimate(flops=flops, bytes_accessed=size, transcendentals=0),
    )(*args)


def matmul(left, right, lc=1, rc=0):
    return lax.dot_general(
        left, right, (((lc,), (rc,)), ((), ())), precision=HIGH, preferred_element_type=F32
    )


def half_dot(left, right, lc=1, rc=0):
    return lax.dot_general(
        left, right, (((lc,), (rc,)), ((), ())), preferred_element_type=F32
    )


def to_owners():
    s = np.zeros((NZ * PAD, 3 * BLK), np.float32)
    for z in range(NZ):
        for m in range(3):
            for i in range(OWN):
                s[z * PAD + m * OWN + i, m * BLK + z * OWN + i] = 1
    return s


def join_cores(index, a0, a1, a2, r0, r1, r2, out):
    core = index[0]
    for m, (a, r) in enumerate(((a0, r0), (a1, r1), (a2, r2))):

        def body(k, _, a=a, r=r, m=m):
            out[k, m] = (a[core, k].astype(F32) + r[k].astype(F32)).astype(BF16)
            return 0

        lax.fori_loop(0, XY, body, 0)


def join_blocks(parts, sel, out):
    rows = []
    for m in range(3):
        total = parts[0, m].astype(F32)
        for k in range(1, XY):
            total += parts[k, m].astype(F32)
        rows.append(total)
    block = jnp.concatenate(rows, axis=0).astype(BF16)
    moved = jnp.dot(sel[...], block, preferred_element_type=F32).astype(BF16)
    for z in range(NZ):
        out[z] = moved[z * PAD : (z + 1) * PAD]


def own_sum(parts):
    total = parts[0].astype(F32)
    for z in range(1, NZ):
        total += parts[z].astype(F32)
    return total


def step_kernel(parts, w_rows, out, grad, scale):
    total = own_sum(parts)
    s = jnp.sqrt(jnp.sum(total * total, axis=1, keepdims=True) / D + EPSILON)
    fast = (w_rows[...] - STEP_SIZE * total / s).astype(BF16)
    for z in range(NZ):
        out[z] = fast
    grad[...] = total
    scale[...] = jnp.broadcast_to(s, scale.shape)


def back_kernel(parts, grad, scale, out):
    total = own_sum(parts)
    g = grad[...]
    s = scale[:, 0:1]
    product = jnp.sum(-STEP_SIZE * total * g, axis=1, keepdims=True)
    cot = (-STEP_SIZE * total / s - g * product / (D * s * s * s)).astype(BF16)
    for z in range(NZ):
        out[z] = cot


def last_kernel(parts, out):
    total = own_sum(parts) * (1.0 / 32768)
    for y in range(NY):
        out[y] = total


def spread_block(parts, sel, out):
    owners = jnp.concatenate([parts[z] for z in range(NZ)], axis=0)
    block = lax.dot_general(
        sel[...], owners, (((0,), (0,)), ((), ())), preferred_element_type=F32
    ).astype(BF16)
    for m in range(3):
        rows = block[m * BLK : (m + 1) * BLK]
        for k in range(XY):
            out[k, m] = rows


def assemble(index, mine, other, o0, o1, o2):
    core = index[0]
    for m, o in enumerate((o0, o1, o2)):

        def body(k, _, o=o, m=m):
            o[core, k] = mine[k, m]
            o[1 - core, k] = other[k, m]
            return 0

        lax.fori_loop(0, XY, body, 0)


def swap_core(a):
    return lax.ppermute(a, "c", [(0, 1), (1, 0)])


def exchange(a, axis):
    return lax.all_to_all(a, axis, split_axis=0, concat_axis=0, tiled=True)


def to_other_core(total, core):
    half = total.reshape(NC, XY, BLK, D)
    return half, swap_core(lax.dynamic_index_in_dim(half, 1 - core, 0, keepdims=False))


def reduce_to_owners(totals, core, index, sel):
    halves = [to_other_core(t, core) for t in totals]
    (joined,) = call(
        join_cores,
        [((XY, 3, BLK, D), BF16)],
        index,
        *(h for h, _ in halves),
        *(r for _, r in halves),
        scalars=1,
    )
    arrived = exchange(joined, ("x", "y"))
    (blocks,) = call(join_blocks, [((NZ, PAD, D), BF16)], arrived, sel)
    return exchange(blocks, "z")


def spread_from_owners(copies, index, sel):
    arrived = exchange(copies, "z")
    (blocks,) = call(spread_block, [((XY, 3, BLK, D), BF16)], arrived, sel)
    mine = exchange(blocks, ("x", "y"))
    other = swap_core(mine)
    outs = call(
        assemble, [((NC, XY, BLK, D), BF16)] * 3, index, mine, other, scalars=1
    )
    return tuple(o.reshape(D, D) for o in outs)


def on_device(queries, key_tokens, values, out_grad, w_gate, w_up, w_down):
    cy, cz, cx, cc = (lax.axis_index(a) for a in ("y", "z", "x", "c"))
    index = jnp.stack([cc, cx, cy, cz]).astype(jnp.int32)
    sel = jnp.asarray(to_owners(), BF16)

    base = ((cc * NX + cx) * NY + cy) * BLK + cz * OWN
    row = lax.broadcasted_iota(jnp.int32, (PAD, D), 0)
    col = lax.broadcasted_iota(jnp.int32, (PAD, D), 1)
    w_rows = 0.0
    for m, w in enumerate((w_gate, w_up, w_down)):
        pick = (col == base + row - m * OWN) & (row >= m * OWN) & (row < (m + 1) * OWN)
        w_rows = w_rows + matmul(pick.astype(F32), w, 1, 1)

    g = matmul(key_tokens, w_gate)
    u = matmul(key_tokens, w_up)
    s = jax.nn.sigmoid(g)
    f = g * s
    f1 = s * (1.0 + g * (1.0 - s))
    a = f * u
    e = matmul(a, w_down) - values
    grad_down = matmul(e, a, 0, 0).astype(BF16)
    da = matmul(e, w_down, 1, 1)
    du = da * f
    dg = da * u * f1
    grad_gate = matmul(dg, key_tokens, 0, 0).astype(BF16)
    grad_up = matmul(du, key_tokens, 0, 0).astype(BF16)
    parts = reduce_to_owners((grad_gate, grad_up, grad_down), cc, index, sel)

    copies, grad, scale = call(
        step_kernel,
        [((NZ, PAD, D), BF16), ((PAD, D), F32), ((PAD, 128), F32)],
        parts,
        w_rows,
    )
    p_t, q_t, r_t = spread_from_owners(copies, index, sel)

    hg = half_dot(queries, p_t, 1, 1)
    hu = half_dot(queries, q_t, 1, 1)
    sq = jax.nn.sigmoid(hg)
    act = (hg * sq * hu).astype(BF16)
    dact = half_dot(out_grad, r_t, 1, 0)
    du_q = (dact * hg * sq).astype(BF16)
    dg_q = (dact * hu * sq * (1.0 + hg * (1.0 - sq))).astype(BF16)
    h_gate = half_dot(dg_q, queries, 0, 0).astype(BF16)
    h_up = half_dot(du_q, queries, 0, 0).astype(BF16)
    h_down = half_dot(out_grad, act, 0, 0).astype(BF16)
    d_queries = (half_dot(dg_q, p_t, 1, 0) + half_dot(du_q, q_t, 1, 0)).astype(BF16)
    parts = reduce_to_owners((h_gate, h_up, h_down), cc, index, sel)

    (copies,) = call(back_kernel, [((NZ, PAD, D), BF16)], parts, grad, scale)
    cot = spread_from_owners(copies, index, sel)
    ga_t, ua_t, da_t = (t.astype(F32) for t in cot)

    t_dg = matmul(key_tokens, ga_t, 1, 1)
    t_du = matmul(key_tokens, ua_t, 1, 1)
    f2 = s * (1.0 - s) * (2.0 + g * (1.0 - 2.0 * s))
    da_cot = t_dg * u * f1 + t_du * f
    e_cot = matmul(a, da_t, 1, 1) + matmul(da_cot, w_down, 1, 0)
    a_cot = matmul(e, da_t, 1, 0) + matmul(e_cot, w_down, 1, 1)
    u_cot = t_dg * da * f1 + a_cot * f
    g_cot = t_dg * da * u * f2 + t_du * da * f1 + a_cot * u * f1
    d_keys = (
        matmul(dg, ga_t, 1, 0)
        + matmul(du, ua_t, 1, 0)
        + matmul(g_cot, w_gate, 1, 1)
        + matmul(u_cot, w_up, 1, 1)
    )
    d_values = -e_cot

    order = np.zeros((D, D), np.float32)
    for c in range(NC):
        for x in range(NX):
            for y in range(NY):
                for z in range(NZ):
                    for i in range(OWN):
                        at = ((c * NX + x) * NY + y) * BLK + z * OWN + i
                        order[((z * NX + x) * NC + c) * 12 + y * OWN + i, at] = 1
    order16 = jnp.asarray(order, BF16)
    order32 = order16.astype(F32)
    keys_o = matmul(key_tokens, order32)
    queries_o = half_dot(queries, order16).astype(BF16)
    a_o = matmul(a, order32)
    act_o = half_dot(act, order16).astype(BF16)
    da_cot_o = matmul(da_cot, order32)
    sum_gate = (matmul(keys_o, g_cot, 0, 0) + half_dot(queries_o, dg_q, 0, 0)).astype(BF16)
    sum_up = (matmul(keys_o, u_cot, 0, 0) + half_dot(queries_o, du_q, 0, 0)).astype(BF16)
    sum_down = (
        matmul(a_o, e_cot, 0, 0) + matmul(da_cot_o, e, 0, 0) + half_dot(act_o, out_grad, 0, 0)
    ).astype(BF16)
    parts = reduce_to_owners((sum_gate, sum_up, sum_down), cc, index, sel)
    (copies,) = call(last_kernel, [((NY, PAD, D), F32)], parts)
    final = exchange(copies, "y")
    out = [
        final[:, m * OWN : (m + 1) * OWN].reshape(NY * OWN, D) for m in range(3)
    ]
    return (d_queries, d_keys, d_values, *out)


def solution(mesh):
    split = Mesh(mesh.devices.reshape(NY, NZ, NX, NC), ("y", "z", "x", "c"))
    rows = P(("y", "z", "x", "c"), None)
    tok = P(("z", "x", "c"), None)
    return jax.shard_map(
        on_device,
        mesh=split,
        in_specs=(rows, rows, rows, rows, P(), P(), P()),
        out_specs=(rows, rows, rows, tok, tok, tok),
        check_vma=False,
    )
```

```python
import jax
import jax.numpy as jnp
import numpy as np
from jax import lax
from jax.experimental import pallas as pl
from jax.experimental.pallas import tpu as pltpu
from jax.sharding import Mesh, PartitionSpec as P

STEP_SIZE = 0.02
EPSILON = 1e-06
F32 = jnp.float32
BF16 = jnp.bfloat16

NY, NZ, NX, NC = 4, 8, 4, 2
D = 768
TOKENS = 32768
WIDE = D // NX
BLK = WIDE // (NC * NY)
OWN = BLK // NZ
PAD = 16
ROWS = NY * OWN

VM = pl.BlockSpec(memory_space=pltpu.VMEM)
SM = pl.BlockSpec(memory_space=pltpu.SMEM)


def call(kernel, outs, *args, scalars=0, flops=0):
    outs = tuple(jax.ShapeDtypeStruct(s, d) for s, d in outs)
    size = sum(int(np.prod(a.shape)) * a.dtype.itemsize for a in (*args, *outs))
    return pl.pallas_call(
        kernel,
        out_shape=outs,
        in_specs=[SM] * scalars + [VM] * (len(args) - scalars),
        out_specs=tuple(VM for _ in outs),
        compiler_params=pltpu.CompilerParams(vmem_limit_bytes=40 * 1024 * 1024),
        cost_estimate=pl.CostEstimate(flops=flops, bytes_accessed=size, transcendentals=0),
    )(*args)


def dot(left, right, lc=1, rc=0):
    return lax.dot_general(
        left, right, (((lc,), (rc,)), ((), ())), preferred_element_type=F32
    )


def dot16(left, right, lc=1, rc=0):
    return dot(left, right, lc, rc).astype(BF16)


def row_order():
    order = np.zeros((NX, NC, NY, NZ, OWN), np.int64)
    for x in range(NX):
        for c in range(NC):
            for y in range(NY):
                for z in range(NZ):
                    for i in range(OWN):
                        order[x, c, y, z, i] = ((z * NX + x) * NC + c) * ROWS + y * OWN + i
    return order.reshape(-1)


def pick_rows():
    s = np.zeros((D, D), np.float32)
    s[np.arange(D), row_order()] = 1
    return s.reshape(NX, WIDE, D)


def to_owners():
    s = np.zeros((NZ * PAD, 3 * BLK), np.float32)
    for z in range(NZ):
        for m in range(3):
            for i in range(OWN):
                s[z * PAD + m * OWN + i, m * BLK + z * OWN + i] = 1
    return s


def join_cores(index, a0, a1, a2, r0, r1, r2, own, *sends):
    core, y = index[0], index[2]
    for k in range(NY):
        to = lax.rem(y + k, NY)
        for m, (a, r) in enumerate(((a0, r0), (a1, r1), (a2, r2))):
            total = a[core, to].astype(F32) + r[to].astype(F32)
            if k == 0:
                own[m] = total
            else:
                sends[k - 1][m] = total.astype(BF16)


def join_blocks(own, r1, r2, r3, sel, out):
    rows = []
    for m in range(3):
        rows.append(own[m] + r1[m].astype(F32) + r2[m].astype(F32) + r3[m].astype(F32))
    block = jnp.concatenate(rows, axis=0).astype(BF16)
    moved = jnp.dot(sel[...], block, preferred_element_type=F32).astype(BF16)
    for z in range(NZ):
        out[z] = moved[z * PAD : (z + 1) * PAD]


def own_sum(parts):
    total = parts[0].astype(F32)
    for z in range(1, NZ):
        total += parts[z].astype(F32)
    return total


def step_kernel(parts, w_rows, out, grad, scale):
    total = own_sum(parts)
    s = jnp.sqrt(jnp.sum(total * total, axis=1, keepdims=True) / D + EPSILON)
    fast = (w_rows[...] - STEP_SIZE * total / s).astype(BF16)
    for z in range(NZ):
        out[z] = fast
    grad[...] = total
    scale[...] = jnp.broadcast_to(s, scale.shape)


def back_kernel(parts, grad, scale, out):
    total = own_sum(parts)
    g = grad[...]
    s = scale[:, 0:1]
    product = jnp.sum(-STEP_SIZE * total * g, axis=1, keepdims=True)
    cot = (-STEP_SIZE * total / s - g * product / (D * s * s * s)).astype(BF16)
    for z in range(NZ):
        out[z] = cot


def last_kernel(parts, out):
    out[...] = (own_sum(parts) * (1.0 / TOKENS)).astype(BF16)


def final_kernel(own, r1, r2, r3, rows, lanes, o0, o1, o2):
    every = jnp.concatenate([own[...], r1[...], r2[...], r3[...]], axis=0)
    moved = jnp.dot(rows[...], every, preferred_element_type=F32)
    first = moved[: 2 * PAD].astype(BF16)
    both = jnp.dot(first, lanes[...], preferred_element_type=F32)
    o0[...] = both[:ROWS]
    o1[...] = both[PAD : PAD + ROWS]
    o2[...] = moved[2 * PAD : 2 * PAD + ROWS]


def spread_block(parts, sel, out):
    owners = jnp.concatenate([parts[z] for z in range(NZ)], axis=0)
    block = lax.dot_general(
        sel[...], owners, (((0,), (0,)), ((), ())), preferred_element_type=F32
    ).astype(BF16)
    for m in range(3):
        out[m] = block[m * BLK : (m + 1) * BLK]


def assemble(index, *refs):
    core, y = index[0], index[2]
    mine, other, outs = refs[:NY], refs[NY : 2 * NY], refs[2 * NY :]
    for k in range(NY):
        at = lax.rem(y + NY - k, NY)
        for m, o in enumerate(outs):
            o[core, at] = mine[k][m]
            o[1 - core, at] = other[k][m]


def swap_core(a):
    return lax.ppermute(a, "c", [(0, 1), (1, 0)])


def ring(a, axis, step):
    n = lax.axis_size(axis)
    return lax.ppermute(a, axis, [(i, (i + step) % n) for i in range(n)])


def exchange_z(a):
    return lax.all_to_all(a, "z", split_axis=0, concat_axis=0, tiled=True)


def from_ring(a):
    return [a] + [ring(a, "x", k) for k in range(1, NX)]


def back_on_ring(blocks):
    return [blocks[0]] + [ring(blocks[k], "x", -k) for k in range(1, NX)]


def ahead_on_ring(blocks):
    return [blocks[0]] + [ring(blocks[k], "x", k) for k in range(1, NX)]


def own_tokens(partial):
    blocks = partial.reshape(NX, -1, D)
    arrived = back_on_ring([blocks[0]] + [blocks[k].astype(BF16) for k in range(1, NX)])
    total = arrived[0]
    for k in range(1, NX):
        total = total + arrived[k].astype(F32)
    return total


def reduce_to_owners(totals, core, index, sel):
    halves = [t.reshape(NC, NY, BLK, D) for t in totals]
    arrived = [
        swap_core(lax.dynamic_index_in_dim(h, 1 - core, 0, keepdims=False)) for h in halves
    ]
    block = (3, BLK, D)
    own, *sends = call(
        join_cores, [(block, F32)] + [(block, BF16)] * (NY - 1), index, *halves, *arrived, scalars=1
    )
    got = [ring(s, "y", k + 1) for k, s in enumerate(sends)]
    (blocks,) = call(join_blocks, [((NZ, PAD, D), BF16)], own, *got, sel)
    return exchange_z(blocks)


def spread_from_owners(copies, index, sel):
    arrived = exchange_z(copies)
    (block,) = call(spread_block, [((3, BLK, D), BF16)], arrived, sel)
    mine = [block] + [ring(block, "y", k) for k in range(1, NY)]
    other = [swap_core(b) for b in mine]
    outs = call(assemble, [((NC, NY, BLK, D), BF16)] * 3, index, *mine, *other, scalars=1)
    return tuple(o.reshape(WIDE, D) for o in outs)


def on_device(queries, key_tokens, values, out_grad, w_gate, w_up, w_down):
    cy, cz, cx, cc = (lax.axis_index(a) for a in ("y", "z", "x", "c"))
    index = jnp.stack([cc, cx, cy, cz]).astype(jnp.int32)
    sel = jnp.asarray(to_owners(), BF16)

    keys = jnp.concatenate(from_ring(key_tokens.astype(BF16)), axis=0)
    vals = jnp.concatenate(from_ring(values.astype(BF16)), axis=0)
    asks = jnp.concatenate(from_ring(queries), axis=0)
    outg = jnp.concatenate(from_ring(out_grad), axis=0)

    pick = pick_rows()
    twice = jnp.asarray(np.concatenate([pick, pick]).reshape(-1, D), BF16)
    falling = jnp.asarray(
        np.concatenate([pick[-k % NX] for k in range(2 * NX)]).reshape(-1, D), BF16
    )
    ahead = lax.dynamic_slice_in_dim(twice, cx * WIDE, D, 0)
    behind = lax.dynamic_slice_in_dim(falling, lax.rem(NX - cx, NX) * WIDE, D, 0)
    mine = ahead[:WIDE]

    base = ((cz * NX + cx) * NC + cc) * ROWS + cy * OWN
    row = lax.broadcasted_iota(jnp.int32, (PAD, D), 0)
    col = lax.broadcasted_iota(jnp.int32, (PAD, D), 1)
    w_rows = 0.0
    for m, w in enumerate((w_gate, w_up, w_down)):
        at = (col == base + row - m * OWN) & (row >= m * OWN) & (row < (m + 1) * OWN)
        w_rows = w_rows + lax.dot_general(
            at.astype(F32), w, (((1,), (1,)), ((), ())), precision=lax.Precision.HIGHEST
        )

    wa, wb, wc = (w.astype(BF16) for w in (w_gate, w_up, w_down))
    wa_s = dot16(wa, mine, 1, 1)
    wb_s = dot16(wb, mine, 1, 1)
    wc_s = dot16(mine, wc)

    g = dot(keys, wa)
    u = dot(keys, wb)
    a = (g * jax.nn.sigmoid(g) * u).astype(BF16)
    e = (dot(a, wc) - vals.astype(F32)).astype(BF16)
    g = dot(keys, wa_s)
    u = dot(keys, wb_s)
    s = jax.nn.sigmoid(g)
    f = g * s
    f1 = s * (1.0 + g * (1.0 - s))
    a_s = (f * u).astype(BF16)
    da = dot(e, wc_s, 1, 1)
    du = (da * f).astype(BF16)
    dg = (da * u * f1).astype(BF16)
    e_s = dot16(e, mine, 1, 1)
    totals = (dot16(dg, keys, 0, 0), dot16(du, keys, 0, 0), dot16(e_s, a, 0, 0))
    parts = reduce_to_owners(totals, cc, index, sel)

    copies, grad, scale = call(
        step_kernel,
        [((NZ, PAD, D), BF16), ((PAD, D), F32), ((PAD, 128), F32)],
        parts,
        w_rows,
    )
    p_t, q_t, r_t = spread_from_owners(copies, index, sel)

    def my_columns(down_t):
        turned = dot16(down_t, ahead, 1, 1)
        blocks = [turned[:, k * WIDE : (k + 1) * WIDE] for k in range(NX)]
        return jnp.concatenate(ahead_on_ring(blocks), axis=0)

    outg_b = dot16(outg, behind, 1, 1)
    hg = dot(asks, p_t, 1, 1)
    hu = dot(asks, q_t, 1, 1)
    sq = jax.nn.sigmoid(hg)
    act = (hg * sq * hu).astype(BF16)
    h_down = dot16(outg_b, act, 0, 0).reshape(NX, WIDE, WIDE)
    h_down = jnp.concatenate(back_on_ring([h_down[k] for k in range(NX)]), axis=1)
    h_down = dot16(h_down, ahead)
    dact = dot(outg_b, my_columns(r_t))
    du_q = (dact * hg * sq).astype(BF16)
    dg_q = (dact * hu * sq * (1.0 + hg * (1.0 - sq))).astype(BF16)
    totals = (dot16(dg_q, asks, 0, 0), dot16(du_q, asks, 0, 0), h_down)
    d_queries = own_tokens(dot(dg_q, p_t) + dot(du_q, q_t)).astype(BF16)
    parts = reduce_to_owners(totals, cc, index, sel)

    (copies,) = call(back_kernel, [((NZ, PAD, D), BF16)], parts, grad, scale)
    ga_t, ua_t, da_t = spread_from_owners(copies, index, sel)

    t_dg = dot(keys, ga_t, 1, 1)
    t_du = dot(keys, ua_t, 1, 1)
    f2 = s * (1.0 - s) * (2.0 + g * (1.0 - 2.0 * s))
    da_cot = (t_dg * u * f1 + t_du * f).astype(BF16)
    through = jnp.concatenate([da_cot, dot16(a, da_t, 1, 1)], axis=1)
    wc_b = dot16(behind, wc).reshape(NX, WIDE, D)
    spread = jnp.concatenate([wc_b, behind.reshape(NX, WIDE, D)], axis=1)
    tokens = values.shape[0]
    turned = [jnp.roll(b, k * tokens, axis=0) for k, b in enumerate(from_ring(through))]
    e_cot = dot(jnp.concatenate(turned, axis=1), spread.reshape(-1, D))
    e_cot16 = e_cot.astype(BF16)
    e_b = dot16(e, behind, 1, 1)
    a_cot = dot(e_b, my_columns(da_t)) + dot(e_cot16, wc_s, 1, 1)
    u_cot = (t_dg * da * f1 + a_cot * f).astype(BF16)
    g_cot = (t_dg * da * u * f2 + t_du * da * f1 + a_cot * u * f1).astype(BF16)
    d_values = -e_cot[: values.shape[0]]
    d_keys = own_tokens(
        dot(dg, ga_t) + dot(du, ua_t) + dot(g_cot, wa_s, 1, 1) + dot(u_cot, wb_s, 1, 1)
    )

    left = jnp.concatenate([dot16(keys, ahead, 1, 1), dot16(asks, ahead, 1, 1)], axis=0)
    right = jnp.concatenate(
        [jnp.concatenate([g_cot, dg_q], axis=0), jnp.concatenate([u_cot, du_q], axis=0)], axis=1
    )
    both = dot16(left, right, 0, 0).reshape(NX, WIDE, 2 * WIDE)
    both = ahead_on_ring([both[k] for k in range(NX)])
    sum_gate = jnp.concatenate([b[:, :WIDE] for b in both], axis=1)
    sum_up = jnp.concatenate([b[:, WIDE:] for b in both], axis=1)
    sum_down = dot16(
        jnp.concatenate([a_s, da_cot, act], axis=0),
        jnp.concatenate([e_cot16, e, outg], axis=0),
        0,
        0,
    )
    parts = reduce_to_owners((sum_gate, sum_up, sum_down), cc, index, sel)
    (mine_last,) = call(last_kernel, [((PAD, D), BF16)], parts)
    every = [mine_last] + [ring(mine_last, "y", k) for k in range(1, NY)]
    to = lax.broadcasted_iota(jnp.int32, (3 * PAD, NY * PAD), 0)
    at = lax.broadcasted_iota(jnp.int32, (3 * PAD, NY * PAD), 1)
    m, j = to // PAD, to % PAD
    k, r = at // PAD, at % PAD
    there = (j < ROWS) & (j // OWN == (cy + NY - k) % NY) & (r == m * OWN + j % OWN)
    out = call(final_kernel, [((ROWS, D), F32)] * 3, *every, there.astype(BF16), behind)
    return (d_queries, d_keys, d_values, *out)


def solution(mesh):
    split = Mesh(mesh.devices.reshape(NY, NZ, NX, NC), ("y", "z", "x", "c"))
    rows = P(("y", "z", "x", "c"), None)
    tok = P(("z", "x", "c"), None)
    return jax.shard_map(
        on_device,
        mesh=split,
        in_specs=(rows, rows, rows, rows, P(), P(), P()),
        out_specs=(rows, rows, rows, tok, tok, tok),
        check_vma=False,
    )
```

```python
import jax
import jax.numpy as jnp
import numpy as np
from jax import lax
from jax.experimental import pallas as pl
from jax.experimental.pallas import tpu as pltpu
from jax.sharding import Mesh, PartitionSpec as P

STEP_SIZE = 0.02
EPSILON = 1e-06
F32 = jnp.float32
BF16 = jnp.bfloat16

NY, NZ, NX, NC = 4, 8, 4, 2
D = 768
TOKENS = 32768
WIDE = D // NX
BLK = WIDE // (NC * NY)
OWN = BLK // NZ
PAD = 16
ROWS = NY * OWN

VM = pl.BlockSpec(memory_space=pltpu.VMEM)
SM = pl.BlockSpec(memory_space=pltpu.SMEM)


def call(kernel, outs, *args, scalars=0, flops=0, vmem=8):
    outs = tuple(jax.ShapeDtypeStruct(s, d) for s, d in outs)
    size = sum(int(np.prod(a.shape)) * a.dtype.itemsize for a in (*args, *outs))
    return pl.pallas_call(
        kernel,
        out_shape=outs,
        in_specs=[SM] * scalars + [VM] * (len(args) - scalars),
        out_specs=tuple(VM for _ in outs),
        compiler_params=pltpu.CompilerParams(vmem_limit_bytes=vmem * 1024 * 1024),
        cost_estimate=pl.CostEstimate(flops=flops, bytes_accessed=size, transcendentals=0),
    )(*args)


def dot(left, right, lc=1, rc=0):
    return lax.dot_general(
        left, right, (((lc,), (rc,)), ((), ())), preferred_element_type=F32
    )


def dot16(left, right, lc=1, rc=0):
    return dot(left, right, lc, rc).astype(BF16)


def row_order():
    order = np.zeros((NX, NC, NY, NZ, OWN), np.int64)
    for x in range(NX):
        for c in range(NC):
            for y in range(NY):
                for z in range(NZ):
                    for i in range(OWN):
                        order[x, c, y, z, i] = ((z * NX + x) * NC + c) * ROWS + y * OWN + i
    return order.reshape(-1)


def pick_rows():
    s = np.zeros((D, D), np.float32)
    s[np.arange(D), row_order()] = 1
    return s.reshape(NX, WIDE, D)


def to_owners():
    s = np.zeros((NZ * PAD, 3 * BLK), np.float32)
    for z in range(NZ):
        for m in range(3):
            for i in range(OWN):
                s[z * PAD + m * OWN + i, m * BLK + z * OWN + i] = 1
    return s


def join_cores(index, a0, a1, a2, r0, r1, r2, own, *sends):
    core, y = index[0], index[2]
    for k in range(NY):
        to = lax.rem(y + k, NY)
        for m, (a, r) in enumerate(((a0, r0), (a1, r1), (a2, r2))):
            total = a[core, to].astype(F32) + r[to].astype(F32)
            if k == 0:
                own[m] = total
            else:
                sends[k - 1][m] = total.astype(BF16)


def join_blocks(own, r1, r2, r3, sel, out):
    rows = []
    for m in range(3):
        rows.append(own[m] + r1[m].astype(F32) + r2[m].astype(F32) + r3[m].astype(F32))
    block = jnp.concatenate(rows, axis=0).astype(BF16)
    moved = jnp.dot(sel[...], block, preferred_element_type=F32).astype(BF16)
    for z in range(NZ):
        out[z] = moved[z * PAD : (z + 1) * PAD]


def own_sum(parts):
    total = parts[0].astype(F32)
    for z in range(1, NZ):
        total += parts[z].astype(F32)
    return total


def step_kernel(parts, w_rows, out, grad, scale):
    total = own_sum(parts)
    s = jnp.sqrt(jnp.sum(total * total, axis=1, keepdims=True) / D + EPSILON)
    fast = (w_rows[...] - STEP_SIZE * total / s).astype(BF16)
    for z in range(NZ):
        out[z] = fast
    grad[...] = total
    scale[...] = jnp.broadcast_to(s, scale.shape)


def back_kernel(parts, grad, scale, out):
    total = own_sum(parts)
    g = grad[...]
    s = scale[:, 0:1]
    product = jnp.sum(-STEP_SIZE * total * g, axis=1, keepdims=True)
    cot = (-STEP_SIZE * total / s - g * product / (D * s * s * s)).astype(BF16)
    for z in range(NZ):
        out[z] = cot


def last_kernel(parts, out):
    out[...] = (own_sum(parts) * (1.0 / TOKENS)).astype(BF16)


def final_kernel(own, r1, r2, r3, rows, place, behind, o0, o1, o2):
    every = jnp.concatenate([own[...], r1[...], r2[...], r3[...]], axis=0)
    moved = jnp.dot(rows[...], every, preferred_element_type=F32)
    both = [moved[:PAD].astype(BF16), moved[PAD : 2 * PAD].astype(BF16)]
    for m, o in enumerate((o0, o1)):
        total = 0.0
        for k in range(NX):
            at = 2 * WIDE * (k % 2)
            part = nt(both[k // 2][:, at : at + 2 * WIDE], place[m]).astype(BF16)
            total += nn(part, behind[k])
        o[...] = total[:ROWS]
    o2[...] = moved[2 * PAD : 2 * PAD + ROWS]


def spread_block(parts, sel, out):
    owners = jnp.concatenate([parts[z] for z in range(NZ)], axis=0)
    block = lax.dot_general(
        sel[...], owners, (((0,), (0,)), ((), ())), preferred_element_type=F32
    ).astype(BF16)
    for m in range(3):
        out[m] = block[m * BLK : (m + 1) * BLK]


def assemble(index, *refs):
    core, y = index[0], index[2]
    mine, other, outs = refs[:NY], refs[NY : 2 * NY], refs[2 * NY :]
    for k in range(NY):
        at = lax.rem(y + NY - k, NY)
        for m, o in enumerate(outs):
            o[core, at] = mine[k][m]
            o[1 - core, at] = other[k][m]


NT = (((1,), (1,)), ((), ()))
TN = (((0,), (0,)), ((), ()))


def nn(left, right):
    return jnp.dot(left, right, preferred_element_type=F32)


def nt(left, right):
    return lax.dot_general(left, right, NT, preferred_element_type=F32)


def tn(left, right):
    return lax.dot_general(left, right, TN, preferred_element_type=F32)


def p1_open(x0, x1, x2, x3, w_gate, w_up, w_down, mine, keys, a, a_s, f, k1, f1, uf2, wa_t, wb_t, wc, wc_s):
    wa, wb = w_gate[...].astype(BF16), w_up[...].astype(BF16)
    wc[...] = w_down[...].astype(BF16)
    wa_t[...] = nt(mine[...], wa).astype(BF16)
    wb_t[...] = nt(mine[...], wb).astype(BF16)
    wc_s[...] = nn(mine[...], wc[...]).astype(BF16)
    rows = jnp.concatenate([x0[...], x1[...], x2[...], x3[...]], axis=0)
    keys[...] = rows
    g = nn(rows, wa)
    a[...] = (g * jax.nn.sigmoid(g) * nn(rows, wb)).astype(BF16)
    g = nt(rows, wa_t[...])
    u = nt(rows, wb_t[...])
    s = jax.nn.sigmoid(g)
    slope = s * (1.0 + g * (1.0 - s))
    f[...] = g * s
    f1[...] = slope
    k1[...] = u * slope
    uf2[...] = u * (s * (1.0 - s) * (2.0 + g * (1.0 - 2.0 * s)))
    a_s[...] = (g * s * u).astype(BF16)


def p1_close(keys, y0, y1, y2, y3, a, wc, wc_s, mine, f, k1, f1, uf2, e, k3, k4, du, dg, t0, t1, t2):
    rows = jnp.concatenate([y0[...], y1[...], y2[...], y3[...]], axis=0).astype(F32)
    err = (nn(a[...], wc[...]) - rows).astype(BF16)
    e[...] = err
    da = nt(err, wc_s[...])
    k3[...] = da * f1[...]
    k4[...] = da * uf2[...]
    up = (da * f[...]).astype(BF16)
    gate = (da * k1[...]).astype(BF16)
    du[...] = up
    dg[...] = gate
    t0[...] = tn(gate, keys[...]).astype(BF16)
    t1[...] = tn(up, keys[...]).astype(BF16)
    e_s = nt(err, mine[...]).astype(BF16)
    t2[...] = tn(e_s, a[...]).astype(BF16)


def p2_gather(b0, b1, b2, b3, behind, asks, outg, outg_b):
    half = b0.shape[0] // 2
    asks[...] = jnp.concatenate([b[:half] for b in (b0, b1, b2, b3)], axis=0)
    rows = jnp.concatenate([b[half:] for b in (b0, b1, b2, b3)], axis=0)
    outg[...] = rows
    outg_b[...] = nt(rows, behind[...]).astype(BF16)


def turn(down_t, ahead, *outs):
    for k, o in enumerate(outs):
        o[...] = nt(down_t[...], ahead[k]).astype(BF16)


def p2_open(asks, p_t, q_t, outg_b, act, hs, hd, *blocks):
    hg = nt(asks[...], p_t[...])
    hu = nt(asks[...], q_t[...])
    sq = jax.nn.sigmoid(hg)
    rounded = (hg * sq * hu).astype(BF16)
    act[...] = rounded
    hs[...] = hg * sq
    hd[...] = hu * sq * (1.0 + hg * (1.0 - sq))
    down = tn(outg_b[...], rounded).astype(BF16)
    for k, o in enumerate(blocks):
        o[...] = down[k * WIDE : (k + 1) * WIDE]


def p2_close(d0, d1, d2, d3, outg_b, hs, hd, asks, h0, h1, h2, h3, ahead, du, dg, t0, t1, t2):
    down = jnp.concatenate([d0[...], d1[...], d2[...], d3[...]], axis=0)
    dact = nn(outg_b[...], down)
    up = (dact * hs[...]).astype(BF16)
    gate = (dact * hd[...]).astype(BF16)
    du[...] = up
    dg[...] = gate
    t0[...] = tn(gate, asks[...]).astype(BF16)
    t1[...] = tn(up, asks[...]).astype(BF16)
    total = nn(h0[...], ahead[0])
    for k, h in enumerate((h1, h2, h3)):
        total += nn(h[...], ahead[k + 1])
    t2[...] = total.astype(BF16)


def p3_open(keys, a, ga_t, ua_t, da_t, place, f, k1, k3, k4, through, da_cot, base_u, base_g):
    t_dg = nt(keys[...], ga_t[...])
    t_du = nt(keys[...], ua_t[...])
    cot = (t_dg * k1[...] + t_du * f[...]).astype(BF16)
    da_cot[...] = cot
    base_u[...] = t_dg * k3[...]
    base_g[...] = t_dg * k4[...] + t_du * k3[...]
    low = jnp.concatenate([jnp.zeros_like(da_t[...]), da_t[...]], axis=0)
    through[...] = (nt(a[...], low) + nn(cot, place[0])).astype(BF16)


def p3_close(t0, t1, t2, t3, spread, d0, d1, d2, d3, e_b, wc_s, place, f, k1, base_u, base_g,
             keys_a, a_s, part_gu, part_down, d_values, gu, down_sum, *blocks):
    step = d_values.shape[0]
    total = [0.0] * NX
    for k, t in enumerate((t0, t1, t2, t3)):
        product = nn(t[...], spread[k])
        for b in range(NX):
            at = (b - k) % NX
            total[b] = total[b] + product[at * step : (at + 1) * step]
    d_values[...] = -total[0]
    e_cot = jnp.concatenate([b.astype(BF16) for b in total], axis=0)
    down = jnp.concatenate([d0[...], d1[...], d2[...], d3[...]], axis=0)
    a_cot = nn(e_b[...], down) + nt(e_cot, wc_s[...])
    u_cot = (base_u[...] + a_cot * f[...]).astype(BF16)
    g_cot = (base_g[...] + a_cot * k1[...]).astype(BF16)
    pair = (nn(g_cot, place[0]) + nn(u_cot, place[1])).astype(BF16)
    gu[...] = pair
    both = (tn(keys_a[...], pair) + part_gu[...]).astype(BF16)
    for k, o in enumerate(blocks):
        o[...] = both[k * WIDE : (k + 1) * WIDE]
    down_sum[...] = (tn(a_s[...], e_cot) + part_down[...]).astype(BF16)


def pick_kernel(index, w_gate, w_up, w_down, out):
    core, x, y, z = index[0], index[1], index[2], index[3]
    base = ((z * NX + x) * NC + core) * ROWS + y * OWN
    row = lax.broadcasted_iota(jnp.int32, (PAD, D), 0)
    col = lax.broadcasted_iota(jnp.int32, (PAD, D), 1)
    total = 0.0
    for m, w in enumerate((w_gate, w_up, w_down)):
        at = (col == base + row - m * OWN) & (row >= m * OWN) & (row < (m + 1) * OWN)
        at = jnp.where(at, 1.0, 0.0).astype(BF16)
        high = w[...].astype(BF16)
        rest = w[...] - high.astype(F32)
        middle = rest.astype(BF16)
        low = (rest - middle.astype(F32)).astype(BF16)
        total += (nt(at, low) + nt(at, middle)) + nt(at, high)
    out[...] = total


def prepare(e, keys, asks, wc, behind, ahead, spread, e_b, keys_a, asks_a):
    for k in range(NX):
        spread[k, :WIDE] = nn(behind[k * WIDE : (k + 1) * WIDE], wc[...]).astype(BF16)
        spread[k, WIDE:] = behind[k * WIDE : (k + 1) * WIDE]
    e_b[...] = nt(e[...], behind[...]).astype(BF16)
    keys_a[...] = nt(keys[...], ahead[...]).astype(BF16)
    asks_a[...] = nt(asks[...], ahead[...]).astype(BF16)


def store_blocks(total, own, sends):
    step = own.shape[0]
    own[...] = total[:step]
    for k, o in enumerate(sends):
        o[...] = total[(k + 1) * step : (k + 2) * step].astype(BF16)


def query_rows(dg, du, p_t, q_t, own, *sends):
    store_blocks(nn(dg[...], p_t[...]) + nn(du[...], q_t[...]), own, sends)


def meanwhile(asks_a, dg_q, du_q, place, da_cot, e, act, outg, dg, du, ga_t, ua_t, part_gu, part_down, part_dk):
    pair = (nn(dg_q[...], place[0]) + nn(du_q[...], place[1])).astype(BF16)
    part_gu[...] = tn(asks_a[...], pair)
    part_down[...] = tn(da_cot[...], e[...]) + tn(act[...], outg[...])
    part_dk[...] = nn(dg[...], ga_t[...]) + nn(du[...], ua_t[...])


def key_rows(gu, wa_t, wb_t, part_dk, own, *sends):
    both = jnp.concatenate([wa_t[...], wb_t[...]], axis=0)
    store_blocks(nn(gu[...], both) + part_dk[...], own, sends)


def after(value, *others):
    return lax.optimization_barrier((value, others))[0]


def swap_core(a):
    return lax.ppermute(a, "c", [(0, 1), (1, 0)])


def ring(a, axis, step):
    n = lax.axis_size(axis)
    return lax.ppermute(a, axis, [(i, (i + step) % n) for i in range(n)])


def exchange_z(a):
    return lax.all_to_all(a, "z", split_axis=0, concat_axis=0, tiled=True)


def from_ring(a):
    return [a] + [ring(a, "x", k) for k in range(1, NX)]


def back_on_ring(blocks):
    return [blocks[0]] + [ring(blocks[k], "x", -k) for k in range(1, NX)]


def ahead_on_ring(blocks):
    return [blocks[0]] + [ring(blocks[k], "x", k) for k in range(1, NX)]


def own_tokens(own, *sends):
    for r in back_on_ring([own, *sends])[1:]:
        own = own + r.astype(F32)
    return own


def reduce_to_blocks(totals, core, index, sel):
    halves = [t.reshape(NC, NY, BLK, D) for t in totals]
    arrived = [
        swap_core(lax.dynamic_index_in_dim(h, 1 - core, 0, keepdims=False)) for h in halves
    ]
    block = (3, BLK, D)
    own, *sends = call(
        join_cores, [(block, F32)] + [(block, BF16)] * (NY - 1), index, *halves, *arrived, scalars=1
    )
    got = [ring(s, "y", k + 1) for k, s in enumerate(sends)]
    (blocks,) = call(join_blocks, [((NZ, PAD, D), BF16)], own, *got, sel)
    return blocks


def spread_from_owners(copies, index, sel):
    arrived = exchange_z(copies)
    (block,) = call(spread_block, [((3, BLK, D), BF16)], arrived, sel)
    mine = [block] + [ring(block, "y", k) for k in range(1, NY)]
    other = [swap_core(b) for b in mine]
    outs = call(assemble, [((NC, NY, BLK, D), BF16)] * 3, index, *mine, *other, scalars=1)
    return tuple(o.reshape(WIDE, D) for o in outs)


def on_device(queries, key_tokens, values, out_grad, w_gate, w_up, w_down):
    cy, cz, cx, cc = (lax.axis_index(a) for a in ("y", "z", "x", "c"))
    index = jnp.stack([cc, cx, cy, cz]).astype(jnp.int32)
    sel = jnp.asarray(to_owners(), BF16)

    keys = from_ring(key_tokens.astype(BF16))
    vals = from_ring(values.astype(BF16))

    pick = pick_rows()
    twice = jnp.asarray(np.concatenate([pick, pick]).reshape(-1, D), BF16)
    falling = jnp.asarray(
        np.concatenate([pick[-k % NX] for k in range(2 * NX)]).reshape(-1, D), BF16
    )
    ahead = lax.dynamic_slice_in_dim(twice, cx * WIDE, D, 0)
    behind = lax.dynamic_slice_in_dim(falling, lax.rem(NX - cx, NX) * WIDE, D, 0)
    mine = ahead[:WIDE]

    count, tokens = NX * values.shape[0], values.shape[0]
    slim = (count, WIDE)
    full = (count, D)
    some = (WIDE, D)
    keys, a, a_s, f, k1, f1, uf2, wa_t, wb_t, wc, wc_s = call(
        p1_open,
        [(full, BF16), (full, BF16), (slim, BF16)] + [(slim, F32)] * 4
        + [(some, BF16), (some, BF16), ((D, D), BF16), (some, BF16)],
        *keys, w_gate, w_up, w_down, mine, flops=2 * count * D * (2 * D + 2 * WIDE), vmem=16,
    )
    e, k3, k4, du, dg, *totals = call(
        p1_close, [(full, BF16)] + [(slim, F32)] * 2 + [(slim, BF16)] * 2 + [(some, BF16)] * 3,
        keys, *vals, a, wc, wc_s, mine, f, k1, f1, uf2, flops=2 * count * D * (D + 5 * WIDE), vmem=16,
    )

    blocks = reduce_to_blocks(totals, cc, index, sel)
    (w_rows,) = call(
        pick_kernel, [((PAD, D), F32)], after(index, blocks), w_gate, w_up, w_down,
        scalars=1, flops=2 * 9 * PAD * D * D, vmem=12,
    )
    pair = jnp.concatenate(after((queries, out_grad), blocks), axis=0)
    parts = exchange_z(blocks)
    asks, outg, outg_b = call(
        p2_gather, [(full, BF16)] * 3, *from_ring(pair), behind, flops=2 * count * D * D
    )
    ahead3 = ahead.reshape(NX, WIDE, D)

    copies, grad, scale = call(
        step_kernel,
        [((NZ, PAD, D), BF16), ((PAD, D), F32), ((PAD, 128), F32)],
        parts,
        w_rows,
    )
    p_t, q_t, r_t = spread_from_owners(copies, index, sel)

    square = ((WIDE, WIDE), BF16)

    def my_columns(down_t):
        return ahead_on_ring(call(turn, [square] * NX, down_t, ahead3, flops=2 * WIDE * D * D))

    down_parts = my_columns(r_t)
    act, hs, hd, *h_down = call(
        p2_open, [(slim, BF16), (slim, F32), (slim, F32)] + [square] * NX,
        asks, p_t, q_t, outg_b, flops=2 * count * D * 3 * WIDE,
    )
    du_q, dg_q, *totals = call(
        p2_close, [(slim, BF16)] * 2 + [(some, BF16)] * 3,
        *down_parts, outg_b, hs, hd, asks, *back_on_ring(h_down), ahead3,
        flops=2 * count * D * 4 * WIDE, vmem=12,
    )
    blocks = reduce_to_blocks(totals, cc, index, sel)
    parts = exchange_z(blocks)
    shares = [((tokens, D), F32)] + [((tokens, D), BF16)] * (NX - 1)
    dg_l, du_l = after((dg_q, du_q), blocks)
    d_queries = own_tokens(
        *call(query_rows, shares, dg_l, du_l, p_t, q_t, flops=4 * count * D * WIDE)
    ).astype(BF16)
    spread, e_b, keys_a, asks_a = call(
        prepare, [((NX, 2 * WIDE, D), BF16)] + [(full, BF16)] * 3,
        e, keys, asks, wc, behind, after(ahead, blocks), flops=2 * D * D * (3 * count + D),
    )

    (copies,) = call(back_kernel, [((NZ, PAD, D), BF16)], parts, grad, scale)
    ga_t, ua_t, da_t = spread_from_owners(copies, index, sel)

    eye = np.zeros((2, WIDE, 2 * WIDE), np.float32)
    for half in range(2):
        eye[half, np.arange(WIDE), half * WIDE + np.arange(WIDE)] = 1
    place = jnp.asarray(eye, BF16)
    through, da_cot, base_u, base_g = call(
        p3_open, [((count, 2 * WIDE), BF16), (slim, BF16), (slim, F32), (slim, F32)],
        keys, a, ga_t, ua_t, da_t, place, f, k1, k3, k4, flops=2 * count * D * WIDE * 5,
    )
    part_gu, part_down, part_dk = call(
        meanwhile, [((D, 2 * WIDE), F32), (some, F32), (full, F32)],
        asks_a, dg_q, du_q, place, da_cot, e, act, outg, dg, du, ga_t, ua_t,
        flops=2 * count * D * 6 * WIDE,
    )
    d_values, gu, sum_down, *both = call(
        p3_close,
        [((tokens, D), F32), ((count, 2 * WIDE), BF16), (some, BF16)]
        + [((WIDE, 2 * WIDE), BF16)] * NX,
        *from_ring(through), spread, *my_columns(da_t), e_b, wc_s, place, f, k1, base_u, base_g,
        keys_a, a_s, part_gu, part_down,
        flops=2 * count * D * 16 * WIDE, vmem=12,
    )

    both = ahead_on_ring(both)
    low, high = jnp.concatenate(both[:2], axis=1), jnp.concatenate(both[2:], axis=1)
    blocks = reduce_to_blocks((low, high, sum_down), cc, index, sel)
    parts = exchange_z(blocks)
    d_keys = own_tokens(
        *call(key_rows, shares, after(gu, blocks), wa_t, wb_t, part_dk, flops=4 * count * D * WIDE)
    )
    (mine_last,) = call(last_kernel, [((PAD, D), BF16)], parts)
    every = [mine_last] + [ring(mine_last, "y", k) for k in range(1, NY)]
    to = lax.broadcasted_iota(jnp.int32, (3 * PAD, NY * PAD), 0)
    at = lax.broadcasted_iota(jnp.int32, (3 * PAD, NY * PAD), 1)
    m, j = to // PAD, to % PAD
    k, r = at // PAD, at % PAD
    there = (j < ROWS) & (j // OWN == (cy + NY - k) % NY) & (r == m * OWN + j % OWN)
    out = call(final_kernel, [((ROWS, D), F32)] * 3, *every, there.astype(BF16),
        place, behind.reshape(NX, WIDE, D),
    )
    return (d_queries, d_keys, d_values, *out)


def solution(mesh):
    split = Mesh(mesh.devices.reshape(NY, NZ, NX, NC), ("y", "z", "x", "c"))
    rows = P(("y", "z", "x", "c"), None)
    tok = P(("z", "x", "c"), None)
    return jax.shard_map(
        on_device,
        mesh=split,
        in_specs=(rows, rows, rows, rows, P(), P(), P()),
        out_specs=(rows, rows, rows, tok, tok, tok),
        check_vma=False,
    )
```

```python
import jax
import jax.numpy as jnp
import numpy as np
from jax import lax
from jax.experimental import pallas as pl
from jax.experimental.pallas import tpu as pltpu
from jax.sharding import Mesh, PartitionSpec as P

STEP_SIZE = 0.02
EPSILON = 1e-06
F32 = jnp.float32
BF16 = jnp.bfloat16

NY, NZ, NX, NC = 4, 8, 4, 2
D = 768
TOKENS = 32768
WIDE = D // NX
BLK = WIDE // (NC * NY)
OWN = BLK // NZ
PAD = 16
ROWS = NY * OWN

VM = pl.BlockSpec(memory_space=pltpu.VMEM)
SM = pl.BlockSpec(memory_space=pltpu.SMEM)


def call(kernel, outs, *args, scalars=0, flops=0, vmem=8):
    outs = tuple(jax.ShapeDtypeStruct(s, d) for s, d in outs)
    size = sum(int(np.prod(a.shape)) * a.dtype.itemsize for a in (*args, *outs))
    return pl.pallas_call(
        kernel,
        out_shape=outs,
        in_specs=[SM] * scalars + [VM] * (len(args) - scalars),
        out_specs=tuple(VM for _ in outs),
        compiler_params=pltpu.CompilerParams(vmem_limit_bytes=vmem * 1024 * 1024),
        cost_estimate=pl.CostEstimate(flops=flops, bytes_accessed=size, transcendentals=0),
    )(*args)


def dot(left, right, lc=1, rc=0):
    return lax.dot_general(
        left, right, (((lc,), (rc,)), ((), ())), preferred_element_type=F32
    )


def dot16(left, right, lc=1, rc=0):
    return dot(left, right, lc, rc).astype(BF16)


def row_order():
    order = np.zeros((NX, NC, NY, NZ, OWN), np.int64)
    for x in range(NX):
        for c in range(NC):
            for y in range(NY):
                for z in range(NZ):
                    for i in range(OWN):
                        order[x, c, y, z, i] = ((z * NX + x) * NC + c) * ROWS + y * OWN + i
    return order.reshape(-1)


def pick_rows():
    s = np.zeros((D, D), np.float32)
    s[np.arange(D), row_order()] = 1
    return s.reshape(NX, WIDE, D)


def to_owners():
    s = np.zeros((NZ * PAD, 3 * BLK), np.float32)
    for z in range(NZ):
        for m in range(3):
            for i in range(OWN):
                s[z * PAD + m * OWN + i, m * BLK + z * OWN + i] = 1
    return s


def store_halves(core, m, total, keep, send):
    low, high = total[: WIDE // 2].astype(BF16), total[WIDE // 2 :].astype(BF16)

    @pl.when(core == 0)
    def _():
        keep[m] = low
        send[m] = high

    @pl.when(core == 1)
    def _():
        keep[m] = high
        send[m] = low


def last_halves(index, b0, b1, b2, b3, down, keep, send):
    pairs = ((b0, b1), (b2, b3))
    for m, (left, right) in enumerate(pairs):
        store_halves(index[0], m, jnp.concatenate([left[...], right[...]], axis=1), keep, send)
    store_halves(index[0], 2, down[...], keep, send)


def join_cores(index, keep, other, own, *sends):
    y = index[2]
    for k in range(NY):
        to = lax.rem(y + k, NY)
        for m in range(3):
            total = keep[m, to].astype(F32) + other[m, to].astype(F32)
            if k == 0:
                own[m] = total
            else:
                sends[k - 1][m] = total.astype(BF16)


def join_blocks(own, r1, r2, r3, sel, out):
    rows = []
    for m in range(3):
        rows.append(own[m] + r1[m].astype(F32) + r2[m].astype(F32) + r3[m].astype(F32))
    block = jnp.concatenate(rows, axis=0).astype(BF16)
    moved = jnp.dot(sel[...], block, preferred_element_type=F32).astype(BF16)
    for z in range(NZ):
        out[z] = moved[z * PAD : (z + 1) * PAD]


def own_sum(parts):
    total = parts[0].astype(F32)
    for z in range(1, NZ):
        total += parts[z].astype(F32)
    return total


def step_kernel(parts, w_rows, out, grad, scale):
    total = own_sum(parts)
    s = jnp.sqrt(jnp.sum(total * total, axis=1, keepdims=True) / D + EPSILON)
    fast = (w_rows[...] - STEP_SIZE * total / s).astype(BF16)
    for z in range(NZ):
        out[z] = fast
    grad[...] = total
    scale[...] = jnp.broadcast_to(s, scale.shape)


def back_kernel(parts, grad, scale, out):
    total = own_sum(parts)
    g = grad[...]
    s = scale[:, 0:1]
    product = jnp.sum(-STEP_SIZE * total * g, axis=1, keepdims=True)
    cot = (-STEP_SIZE * total / s - g * product / (D * s * s * s)).astype(BF16)
    for z in range(NZ):
        out[z] = cot


def last_kernel(parts, out):
    out[...] = (own_sum(parts) * (1.0 / TOKENS)).astype(BF16)


def final_kernel(own, r1, r2, r3, rows, place, behind, o0, o1, o2):
    every = jnp.concatenate([own[...], r1[...], r2[...], r3[...]], axis=0)
    moved = jnp.dot(rows[...], every, preferred_element_type=F32)
    both = [moved[:PAD].astype(BF16), moved[PAD : 2 * PAD].astype(BF16)]
    for m, o in enumerate((o0, o1)):
        total = 0.0
        for k in range(NX):
            at = 2 * WIDE * (k % 2)
            part = nt(both[k // 2][:, at : at + 2 * WIDE], place[m]).astype(BF16)
            total += nn(part, behind[k])
        o[...] = total[:ROWS]
    o2[...] = moved[2 * PAD : 2 * PAD + ROWS]


def spread_block(parts, sel, out):
    owners = jnp.concatenate([parts[z] for z in range(NZ)], axis=0)
    block = lax.dot_general(
        sel[...], owners, (((0,), (0,)), ((), ())), preferred_element_type=F32
    ).astype(BF16)
    for m in range(3):
        out[m] = block[m * BLK : (m + 1) * BLK]


def assemble(index, *refs):
    core, y = index[0], index[2]
    mine, other, outs = refs[:NY], refs[NY : 2 * NY], refs[2 * NY :]
    for k in range(NY):
        at = lax.rem(y + NY - k, NY)
        for m, o in enumerate(outs):
            o[core, at] = mine[k][m]
            o[1 - core, at] = other[k][m]


NT = (((1,), (1,)), ((), ()))
TN = (((0,), (0,)), ((), ()))


def nn(left, right):
    return jnp.dot(left, right, preferred_element_type=F32)


def nt(left, right):
    return lax.dot_general(left, right, NT, preferred_element_type=F32)


def tn(left, right):
    return lax.dot_general(left, right, TN, preferred_element_type=F32)


def p1_open(x0, x1, x2, x3, w_gate, w_up, w_down, mine, keys, a, a_s, f, k1, f1, uf2, wa_t, wb_t, wc, wc_s):
    wa, wb = w_gate[...].astype(BF16), w_up[...].astype(BF16)
    wc[...] = w_down[...].astype(BF16)
    wa_t[...] = nt(mine[...], wa).astype(BF16)
    wb_t[...] = nt(mine[...], wb).astype(BF16)
    wc_s[...] = nn(mine[...], wc[...]).astype(BF16)
    rows = jnp.concatenate([x0[...], x1[...], x2[...], x3[...]], axis=0)
    keys[...] = rows
    g = nn(rows, wa)
    a[...] = (g * jax.nn.sigmoid(g) * nn(rows, wb)).astype(BF16)
    g = nt(rows, wa_t[...])
    u = nt(rows, wb_t[...])
    s = jax.nn.sigmoid(g)
    slope = s * (1.0 + g * (1.0 - s))
    f[...] = g * s
    f1[...] = slope
    k1[...] = u * slope
    uf2[...] = u * (s * (1.0 - s) * (2.0 + g * (1.0 - 2.0 * s)))
    a_s[...] = (g * s * u).astype(BF16)


def p1_close(index, keys, y0, y1, y2, y3, a, wc, wc_s, mine, f, k1, f1, uf2, e, k3, k4, du, dg, keep, send):
    rows = jnp.concatenate([y0[...], y1[...], y2[...], y3[...]], axis=0).astype(F32)
    err = (nn(a[...], wc[...]) - rows).astype(BF16)
    e[...] = err
    da = nt(err, wc_s[...])
    k3[...] = da * f1[...]
    k4[...] = da * uf2[...]
    up = (da * f[...]).astype(BF16)
    gate = (da * k1[...]).astype(BF16)
    du[...] = up
    dg[...] = gate
    store_halves(index[0], 0, tn(gate, keys[...]), keep, send)
    store_halves(index[0], 1, tn(up, keys[...]), keep, send)
    e_s = nt(err, mine[...]).astype(BF16)
    store_halves(index[0], 2, tn(e_s, a[...]), keep, send)


def p2_gather(b0, b1, b2, b3, behind, asks, outg, outg_b):
    half = b0.shape[0] // 2
    asks[...] = jnp.concatenate([b[:half] for b in (b0, b1, b2, b3)], axis=0)
    rows = jnp.concatenate([b[half:] for b in (b0, b1, b2, b3)], axis=0)
    outg[...] = rows
    outg_b[...] = nt(rows, behind[...]).astype(BF16)


def turn(down_t, ahead, *outs):
    for k, o in enumerate(outs):
        o[...] = nt(down_t[...], ahead[k]).astype(BF16)


def p2_open(asks, p_t, q_t, outg_b, act, hs, hd, *blocks):
    hg = nt(asks[...], p_t[...])
    hu = nt(asks[...], q_t[...])
    sq = jax.nn.sigmoid(hg)
    rounded = (hg * sq * hu).astype(BF16)
    act[...] = rounded
    hs[...] = hg * sq
    hd[...] = hu * sq * (1.0 + hg * (1.0 - sq))
    down = tn(outg_b[...], rounded).astype(BF16)
    for k, o in enumerate(blocks):
        o[...] = down[k * WIDE : (k + 1) * WIDE]


def p2_close(index, d0, d1, d2, d3, outg_b, hs, hd, asks, h0, h1, h2, h3, ahead, du, dg, keep, send):
    down = jnp.concatenate([d0[...], d1[...], d2[...], d3[...]], axis=0)
    dact = nn(outg_b[...], down)
    up = (dact * hs[...]).astype(BF16)
    gate = (dact * hd[...]).astype(BF16)
    du[...] = up
    dg[...] = gate
    store_halves(index[0], 0, tn(gate, asks[...]), keep, send)
    store_halves(index[0], 1, tn(up, asks[...]), keep, send)
    total = nn(h0[...], ahead[0])
    for k, h in enumerate((h1, h2, h3)):
        total += nn(h[...], ahead[k + 1])
    store_halves(index[0], 2, total, keep, send)


def p3_open(keys, a, ga_t, ua_t, da_t, place, f, k1, k3, k4, through, da_cot, base_u, base_g):
    t_dg = nt(keys[...], ga_t[...])
    t_du = nt(keys[...], ua_t[...])
    cot = (t_dg * k1[...] + t_du * f[...]).astype(BF16)
    da_cot[...] = cot
    base_u[...] = t_dg * k3[...]
    base_g[...] = t_dg * k4[...] + t_du * k3[...]
    low = jnp.concatenate([jnp.zeros_like(da_t[...]), da_t[...]], axis=0)
    through[...] = (nt(a[...], low) + nn(cot, place[0])).astype(BF16)


def p3_close(t0, t1, t2, t3, spread, d0, d1, d2, d3, e_b, wc_s, place, f, k1, base_u, base_g,
             keys_a, a_s, part_gu, part_down, d_values, gu, down_sum, *blocks):
    step = d_values.shape[0]
    total = [0.0] * NX
    for k, t in enumerate((t0, t1, t2, t3)):
        product = nn(t[...], spread[k])
        for b in range(NX):
            at = (b - k) % NX
            total[b] = total[b] + product[at * step : (at + 1) * step]
    d_values[...] = -total[0]
    e_cot = jnp.concatenate([b.astype(BF16) for b in total], axis=0)
    down = jnp.concatenate([d0[...], d1[...], d2[...], d3[...]], axis=0)
    a_cot = nn(e_b[...], down) + nt(e_cot, wc_s[...])
    u_cot = (base_u[...] + a_cot * f[...]).astype(BF16)
    g_cot = (base_g[...] + a_cot * k1[...]).astype(BF16)
    pair = (nn(g_cot, place[0]) + nn(u_cot, place[1])).astype(BF16)
    gu[...] = pair
    both = (tn(keys_a[...], pair) + part_gu[...]).astype(BF16)
    for k, o in enumerate(blocks):
        o[...] = both[k * WIDE : (k + 1) * WIDE]
    down_sum[...] = (tn(a_s[...], e_cot) + part_down[...]).astype(BF16)


def pick_kernel(index, w_gate, w_up, w_down, out):
    core, x, y, z = index[0], index[1], index[2], index[3]
    base = ((z * NX + x) * NC + core) * ROWS + y * OWN
    row = lax.broadcasted_iota(jnp.int32, (PAD, D), 0)
    col = lax.broadcasted_iota(jnp.int32, (PAD, D), 1)
    total = 0.0
    for m, w in enumerate((w_gate, w_up, w_down)):
        at = (col == base + row - m * OWN) & (row >= m * OWN) & (row < (m + 1) * OWN)
        at = jnp.where(at, 1.0, 0.0).astype(BF16)
        high = w[...].astype(BF16)
        rest = w[...] - high.astype(F32)
        middle = rest.astype(BF16)
        low = (rest - middle.astype(F32)).astype(BF16)
        total += (nt(at, low) + nt(at, middle)) + nt(at, high)
    out[...] = total


def prepare(e, keys, asks, wc, behind, ahead, spread, e_b, keys_a, asks_a):
    for k in range(NX):
        spread[k, :WIDE] = nn(behind[k * WIDE : (k + 1) * WIDE], wc[...]).astype(BF16)
        spread[k, WIDE:] = behind[k * WIDE : (k + 1) * WIDE]
    e_b[...] = nt(e[...], behind[...]).astype(BF16)
    keys_a[...] = nt(keys[...], ahead[...]).astype(BF16)
    asks_a[...] = nt(asks[...], ahead[...]).astype(BF16)


def store_blocks(total, own, sends):
    step = own.shape[0]
    own[...] = total[:step]
    for k, o in enumerate(sends):
        o[...] = total[(k + 1) * step : (k + 2) * step].astype(BF16)


def query_rows(dg, du, p_t, q_t, own, *sends):
    store_blocks(nn(dg[...], p_t[...]) + nn(du[...], q_t[...]), own, sends)


def meanwhile(asks_a, dg_q, du_q, place, da_cot, e, act, outg, dg, du, ga_t, ua_t, part_gu, part_down, part_dk):
    pair = (nn(dg_q[...], place[0]) + nn(du_q[...], place[1])).astype(BF16)
    part_gu[...] = tn(asks_a[...], pair)
    part_down[...] = tn(da_cot[...], e[...]) + tn(act[...], outg[...])
    part_dk[...] = nn(dg[...], ga_t[...]) + nn(du[...], ua_t[...])


def key_rows(gu, wa_t, wb_t, part_dk, own, *sends):
    both = jnp.concatenate([wa_t[...], wb_t[...]], axis=0)
    store_blocks(nn(gu[...], both) + part_dk[...], own, sends)


def after(value, *others):
    return lax.optimization_barrier((value, others))[0]


def swap_core(a):
    return lax.ppermute(a, "c", [(0, 1), (1, 0)])


def ring(a, axis, step):
    n = lax.axis_size(axis)
    return lax.ppermute(a, axis, [(i, (i + step) % n) for i in range(n)])


def exchange_z(a):
    return lax.all_to_all(a, "z", split_axis=0, concat_axis=0, tiled=True)


def from_ring(a):
    return [a] + [ring(a, "x", k) for k in range(1, NX)]


def back_on_ring(blocks):
    return [blocks[0]] + [ring(blocks[k], "x", -k) for k in range(1, NX)]


def ahead_on_ring(blocks):
    return [blocks[0]] + [ring(blocks[k], "x", k) for k in range(1, NX)]


def own_tokens(own, *sends):
    for r in back_on_ring([own, *sends])[1:]:
        own = own + r.astype(F32)
    return own


def reduce_to_blocks(keep, send, index, sel):
    keep, other = (t.reshape(3, NY, BLK, D) for t in (keep, swap_core(send)))
    block = (3, BLK, D)
    own, *sends = call(
        join_cores, [(block, F32)] + [(block, BF16)] * (NY - 1), index, keep, other, scalars=1
    )
    got = [ring(s, "y", k + 1) for k, s in enumerate(sends)]
    (blocks,) = call(join_blocks, [((NZ, PAD, D), BF16)], own, *got, sel)
    return blocks


def spread_from_owners(copies, index, sel):
    arrived = exchange_z(copies)
    (block,) = call(spread_block, [((3, BLK, D), BF16)], arrived, sel)
    mine = [block] + [ring(block, "y", k) for k in range(1, NY)]
    other = [swap_core(b) for b in mine]
    outs = call(assemble, [((NC, NY, BLK, D), BF16)] * 3, index, *mine, *other, scalars=1)
    return tuple(o.reshape(WIDE, D) for o in outs)


def on_device(queries, key_tokens, values, out_grad, w_gate, w_up, w_down):
    cy, cz, cx, cc = (lax.axis_index(a) for a in ("y", "z", "x", "c"))
    index = jnp.stack([cc, cx, cy, cz]).astype(jnp.int32)
    sel = jnp.asarray(to_owners(), BF16)

    keys = from_ring(key_tokens.astype(BF16))
    vals = from_ring(values.astype(BF16))

    pick = pick_rows()
    twice = jnp.asarray(np.concatenate([pick, pick]).reshape(-1, D), BF16)
    falling = jnp.asarray(
        np.concatenate([pick[-k % NX] for k in range(2 * NX)]).reshape(-1, D), BF16
    )
    ahead = lax.dynamic_slice_in_dim(twice, cx * WIDE, D, 0)
    behind = lax.dynamic_slice_in_dim(falling, lax.rem(NX - cx, NX) * WIDE, D, 0)
    mine = ahead[:WIDE]

    count, tokens = NX * values.shape[0], values.shape[0]
    slim = (count, WIDE)
    full = (count, D)
    some = (WIDE, D)
    split = ((3, WIDE // 2, D), BF16)
    keys, a, a_s, f, k1, f1, uf2, wa_t, wb_t, wc, wc_s = call(
        p1_open,
        [(full, BF16), (full, BF16), (slim, BF16)] + [(slim, F32)] * 4
        + [(some, BF16), (some, BF16), ((D, D), BF16), (some, BF16)],
        *keys, w_gate, w_up, w_down, mine, flops=2 * count * D * (2 * D + 2 * WIDE), vmem=16,
    )
    e, k3, k4, du, dg, *totals = call(
        p1_close, [(full, BF16)] + [(slim, F32)] * 2 + [(slim, BF16)] * 2 + [split] * 2,
        index, keys, *vals, a, wc, wc_s, mine, f, k1, f1, uf2, scalars=1,
        flops=2 * count * D * (D + 5 * WIDE), vmem=16,
    )

    blocks = reduce_to_blocks(*totals, index, sel)
    (w_rows,) = call(
        pick_kernel, [((PAD, D), F32)], after(index, blocks), w_gate, w_up, w_down,
        scalars=1, flops=2 * 9 * PAD * D * D, vmem=12,
    )
    pair = after(jnp.concatenate([queries, out_grad], axis=0), blocks)
    parts = exchange_z(blocks)
    asks, outg, outg_b = call(
        p2_gather, [(full, BF16)] * 3, *from_ring(pair), behind, flops=2 * count * D * D
    )
    ahead3 = ahead.reshape(NX, WIDE, D)

    copies, grad, scale = call(
        step_kernel,
        [((NZ, PAD, D), BF16), ((PAD, D), F32), ((PAD, 128), F32)],
        parts,
        w_rows,
    )
    p_t, q_t, r_t = spread_from_owners(copies, index, sel)

    square = ((WIDE, WIDE), BF16)

    def my_columns(down_t):
        return ahead_on_ring(call(turn, [square] * NX, down_t, ahead3, flops=2 * WIDE * D * D))

    down_parts = my_columns(r_t)
    act, hs, hd, *h_down = call(
        p2_open, [(slim, BF16), (slim, F32), (slim, F32)] + [square] * NX,
        asks, p_t, q_t, outg_b, flops=2 * count * D * 3 * WIDE,
    )
    du_q, dg_q, *totals = call(
        p2_close, [(slim, BF16)] * 2 + [split] * 2,
        index, *down_parts, outg_b, hs, hd, asks, *back_on_ring(h_down), ahead3,
        scalars=1, flops=2 * count * D * 4 * WIDE, vmem=12,
    )
    blocks = reduce_to_blocks(*totals, index, sel)
    parts = exchange_z(blocks)
    shares = [((tokens, D), F32)] + [((tokens, D), BF16)] * (NX - 1)
    dg_l, du_l = after((dg_q, du_q), blocks)
    query_shares = call(query_rows, shares, dg_l, du_l, p_t, q_t, flops=4 * count * D * WIDE)
    grad, scale = after((grad, scale), query_shares)
    d_queries = own_tokens(*query_shares).astype(BF16)
    spread, e_b, keys_a, asks_a = call(
        prepare, [((NX, 2 * WIDE, D), BF16)] + [(full, BF16)] * 3,
        e, keys, asks, wc, behind, after(ahead, blocks), flops=2 * D * D * (3 * count + D),
    )

    (copies,) = call(back_kernel, [((NZ, PAD, D), BF16)], parts, grad, scale)
    ga_t, ua_t, da_t = spread_from_owners(copies, index, sel)

    eye = np.zeros((2, WIDE, 2 * WIDE), np.float32)
    for half in range(2):
        eye[half, np.arange(WIDE), half * WIDE + np.arange(WIDE)] = 1
    place = jnp.asarray(eye, BF16)
    through, da_cot, base_u, base_g = call(
        p3_open, [((count, 2 * WIDE), BF16), (slim, BF16), (slim, F32), (slim, F32)],
        keys, a, ga_t, ua_t, da_t, place, f, k1, k3, k4, flops=2 * count * D * WIDE * 5,
    )
    part_gu, part_down, part_dk = call(
        meanwhile, [((D, 2 * WIDE), F32), (some, F32), (full, F32)],
        asks_a, dg_q, du_q, place, da_cot, e, act, outg, dg, du, ga_t, ua_t,
        flops=2 * count * D * 6 * WIDE,
    )
    d_values, gu, sum_down, *both = call(
        p3_close,
        [((tokens, D), F32), ((count, 2 * WIDE), BF16), (some, BF16)]
        + [((WIDE, 2 * WIDE), BF16)] * NX,
        *from_ring(through), spread, *my_columns(da_t), e_b, wc_s, place, f, k1, base_u, base_g,
        keys_a, a_s, part_gu, part_down,
        flops=2 * count * D * 16 * WIDE, vmem=12,
    )

    both = ahead_on_ring(both)
    totals = call(last_halves, [split] * 2, index, *both, sum_down, scalars=1)
    blocks = reduce_to_blocks(*totals, index, sel)
    parts = exchange_z(blocks)
    d_keys = own_tokens(
        *call(key_rows, shares, after(gu, blocks), wa_t, wb_t, part_dk, flops=4 * count * D * WIDE)
    )
    (mine_last,) = call(last_kernel, [((PAD, D), BF16)], parts)
    every = [mine_last] + [ring(mine_last, "y", k) for k in range(1, NY)]
    to = lax.broadcasted_iota(jnp.int32, (3 * PAD, NY * PAD), 0)
    at = lax.broadcasted_iota(jnp.int32, (3 * PAD, NY * PAD), 1)
    m, j = to // PAD, to % PAD
    k, r = at // PAD, at % PAD
    there = (j < ROWS) & (j // OWN == (cy + NY - k) % NY) & (r == m * OWN + j % OWN)
    out = call(final_kernel, [((ROWS, D), F32)] * 3, *every, there.astype(BF16),
        place, behind.reshape(NX, WIDE, D),
    )
    return (d_queries, d_keys, d_values, *out)


def solution(mesh):
    split = Mesh(mesh.devices.reshape(NY, NZ, NX, NC), ("y", "z", "x", "c"))
    rows = P(("y", "z", "x", "c"), None)
    tok = P(("z", "x", "c"), None)
    return jax.shard_map(
        on_device,
        mesh=split,
        in_specs=(rows, rows, rows, rows, P(), P(), P()),
        out_specs=(rows, rows, rows, tok, tok, tok),
        check_vma=False,
    )
```
